512 devices in a mesh: ship: 64 (over x, z_hi, y), trans: 4 (over z_lo), vert: 2 (over core).
Axes of the slice: x: 4, y: 4, z: 16 (z_hi: 4, z_lo: 4; z = z_hi * 4 + z_lo), core: 2. Of those that a mesh axis runs over, the one named last changes fastest.
Arguments:
- potential: float32 [64, 1024, 512], P('vert', 'ship', 'trans'), may hold values from -6 to 6
- source: float32 [64, 1024, 512], P('vert', 'ship', 'trans'), may hold values from -6 to 6
- stencil: bfloat16 [27, 64, 1024, 512], P(None, 'vert', 'ship', 'trans'), may hold values from -4.6 to 0.1, as said below
- surface_potential: float32 [1024, 512], P(('ship', 'vert'), 'trans'), may hold values from -6 to 6
- elevation: float32 [1024, 512], P(('ship', 'vert'), 'trans'), may hold values from -0.2 to 0.2
- hull_mask: int32 [1024, 512], P(('ship', 'vert'), 'trans'), may hold values 0 or 1
- column_inverse: float32 [2, 64, 64], replicated, may hold values from -0.3 to 0.03
Outputs:
- updated: float32 [64, 1024, 512], P('vert', 'ship', 'trans')
- residual: float32 [64, 1024, 512], P('vert', 'ship', 'trans')
The draws below stay inside these ranges and needn't reach their ends.
Inputs may be any that keep to these rules, and one draw needn't show every extreme that they name: `stencil`: entry 13 of the first dimension (the centre) lies between -4.6 and -3.0 at every cell, the other 26 entries between 0 and 0.1. `hull_mask`: 1 marks a column under a hull panel.
All inputs are finite; a program needn't handle non-finite values. No bound on the sum of `hull_mask` on one device may be relied on, other than what follows from the above.
Results may differ from the reference program's by a relative error of at most 0.0003.
Values may be sent and summed in bfloat16 or wider, within the bound.
A program may use at most 64 MiB of HBM per device.

```python
import jax
import jax.numpy as jnp
from jax import lax

NZ = 64
SWEEPS = 4
NX = 1024
NY = 512


def draw_stencil(key, part):

    def one_offset(offset_index):
        sub_key = jax.random.fold_in(key, offset_index)
        centre_key = jax.random.fold_in(sub_key, 101)
        side_values = jax.random.uniform(sub_key, (NZ, NX, NY), jnp.float32, 0.02, 0.0998)
        centre = jax.random.uniform(centre_key, (NZ, NX, NY), jnp.float32, -4.5, -3.2)
        return jnp.where(offset_index == 13, centre, side_values).astype(jnp.bfloat16)
    return lax.map(one_offset, jnp.arange(27))


def draw_column_inverse(key, part):
    perturbation = 0.006 * jnp.clip(jax.random.normal(key, (2, NZ, NZ), jnp.float32), -5.0, 5.0)
    diagonal_part = jnp.array([-0.27, -0.22], jnp.float32)[:, None, None] * jnp.eye(NZ, dtype=jnp.float32)[None]
    return diagonal_part + perturbation


def touch_ends(values, key, smallest, largest):
    longest = values.shape.index(max(values.shape))
    spots = []
    for shift in (0, 1):
        where = [jax.random.randint(jax.random.fold_in(key, axis), (), 0, length) for axis, length in enumerate(values.shape)]
        where[longest] = (where[longest] + shift) % values.shape[longest]
        spots.append(tuple(where))
    return values.at[spots[0]].set(smallest).at[spots[1]].set(largest)


def block_scale(own_key, extent, shards, least, high):
    def one(position, blocks):
        draws = jax.random.uniform(jax.random.fold_in(jax.random.fold_in(own_key, 6), position), (blocks,), jnp.float32, least / len(shards), high / len(shards))
        return jnp.repeat(jnp.exp(draws), extent[position] // blocks).reshape((-1,) + (1,) * (len(extent) - position - 1))

    factor_of = one(*shards[0])
    for cut in shards[1:]:
        factor_of = factor_of * one(*cut)
    return factor_of


def bell_draw(stream_key, extent, scale, bound, cuts=(), kind=jnp.bfloat16):
    values = scale * jax.random.normal(stream_key, extent, jnp.float32)
    if cuts:
        values = values * block_scale(stream_key, extent, cuts, -0.22, 0.18)
    return jnp.clip(values, -bound, bound).astype(kind)


def setup_inputs(seed: int = 0) -> dict:
    streams_of = jax.random.split(jax.random.key(seed), 8)
    return {
        "potential": bell_draw(streams_of[0], (NZ, NX, NY), 1.0, 6.0, ((0, 2), (1, 64), (2, 4)), jnp.float32),
        "source": bell_draw(streams_of[1], (NZ, NX, NY), 1.0, 6.0, ((0, 2), (1, 64), (2, 4)), jnp.float32),
        "stencil": draw_stencil(jax.random.fold_in(streams_of[7], 71), 0),
        "surface_potential": bell_draw(streams_of[3], (NX, NY), 1.0, 6.0, ((0, 128), (1, 4)), jnp.float32),
        "elevation": jnp.clip(jax.random.uniform(streams_of[4], (NX, NY), jnp.float32, -0.2, 0.2) * block_scale(streams_of[4], (NX, NY), ((0, 128), (1, 4)), -0.4, 0.0), -0.2, 0.2),
        "hull_mask": touch_ends((jax.random.randint(streams_of[5], (NX, NY), 0, 3) < 1).astype(jnp.int32), jax.random.fold_in(streams_of[5], 1), 0, 1),
        "column_inverse": draw_column_inverse(jax.random.fold_in(streams_of[7], 71), 0),
    }


def extend_field(field_values, hull_weight, top_value):
    surface_layer = hull_weight * field_values[-1] + (1.0 - hull_weight) * top_value
    extended = jnp.concatenate([field_values[:1], field_values, surface_layer[None]], axis=0)
    return jnp.pad(extended, ((0, 0), (1, 1), (1, 1)))


def stencil_apply(padded, stencil):
    levels, row_count, col_count = stencil.shape[1], stencil.shape[2], stencil.shape[3]
    summed = jnp.zeros((levels, row_count, col_count), padded.dtype)
    for offset_z in range(3):
        for offset_x in range(3):
            for offset_y in range(3):
                offset_index = 9 * offset_z + 3 * offset_x + offset_y
                window = padded[offset_z:offset_z + levels, offset_x:offset_x + row_count, offset_y:offset_y + col_count]
                summed = summed + stencil[offset_index].astype(padded.dtype) * window
    return summed


def project(column_inverse, hull_weight, weight, vector_field):
    flattened = vector_field.reshape(vector_field.shape[0], -1)
    free_part = jnp.dot(column_inverse[0], flattened, precision=lax.Precision.HIGHEST, preferred_element_type=vector_field.dtype).reshape(vector_field.shape)
    hull_part = jnp.dot(column_inverse[1], flattened, precision=lax.Precision.HIGHEST, preferred_element_type=vector_field.dtype).reshape(vector_field.shape)
    return weight * jnp.where(hull_weight > 0.5, hull_part, free_part)


def reference(potential, source, stencil, surface_potential, elevation, hull_mask, column_inverse):
    hull_weight = hull_mask.astype(potential.dtype)
    applied = stencil_apply(extend_field(potential, hull_weight, surface_potential), stencil)
    residual = source - applied
    weight = 0.5 * (1.0 + elevation) * (1.0 + elevation)
    correction = project(column_inverse, hull_weight, weight, residual)
    zero_top = jnp.zeros_like(surface_potential)
    for sweep_index in range(SWEEPS - 1):
        defect = residual - stencil_apply(extend_field(correction, hull_weight, zero_top), stencil)
        correction = correction + project(column_inverse, hull_weight, weight, defect)
    return potential + correction, residual
```

```python
import jax
import jax.numpy as jnp
from jax import lax
from jax.experimental import pallas as pl
from jax.experimental.pallas import tpu as pltpu
from jax.sharding import PartitionSpec as P

SWEEPS = 4
MESH = pl.DeviceIdType.MESH
F32 = jnp.float32
BF16 = jnp.bfloat16


def kernel(
    pot_hbm, src_hbm, sten_hbm, surf_hbm, elev_hbm, hull_hbm, cinv_hbm,
    upd_hbm, res_hbm,
    pot, srcl, sten, surf, elev, hullm, cinv,
    coef, edge, shifted, field, applied, resid, corr, hull, weight, top, lhs, ghost3, outl,
    rows_s, rows_r, packs_s, packs_r, diag_s, diag_r,
    lsem, xs_sem, xr_sem, row_ss, row_rs, pack_ss, pack_rs, diag_ss, diag_rs, out_ss, out_rs, out_ls,
):
    s = lax.axis_index("ship")
    t = lax.axis_index("trans")
    v = lax.axis_index("vert")
    ships = lax.axis_size("ship")
    transes = lax.axis_size("trans")
    slow_ok = jnp.where(v == 0, s > 0, s < ships - 1)
    role_ok = (slow_ok, s >= 0)
    role_dev = ((s + 2 * v - 1, 1 - v), (s, 1 - v))
    side_ok = (t > 0, t < transes - 1)
    side_t = (t - 1, t + 1)
    edge_x = (7 * v, 7 * (1 - v))
    edge_b = (2 * v, 2 * (1 - v))

    def clear(k, _):
        for role in range(2):
            rows_r[k, role] = jnp.zeros((80, 128), F32)
            packs_r[k, role] = jnp.zeros((8, 128), F32)
            diag_r[k, role] = jnp.zeros((16, 128), F32)
        return 0

    lax.fori_loop(0, SWEEPS, clear, 0)

    barrier = pltpu.get_barrier_semaphore()
    count = 0
    for role in range(2):
        ship, vert = role_dev[role]
        for ok, tt in ((role_ok[role], t), (role_ok[role] & side_ok[0], t - 1), (role_ok[role] & side_ok[1], t + 1)):

            @pl.when(ok)
            def _():
                pl.semaphore_signal(barrier, inc=1, device_id=(ship, tt, vert), device_id_type=MESH)

            count = count + ok.astype(jnp.int32)
    for side in range(2):

        @pl.when(side_ok[side])
        def _():
            pl.semaphore_signal(barrier, inc=1, device_id=(s, side_t[side], v), device_id_type=MESH)

        count = count + side_ok[side].astype(jnp.int32)

    own = pl.ds(pl.multiple_of(8 * v, 8), 8)
    other = pl.ds(pl.multiple_of(8 * (1 - v), 8), 8)
    levels = pl.ds(32 * v, 32)
    local = [
        pltpu.make_async_copy(pot_hbm.at[:, own], pot.at[levels], lsem.at[0]),
        pltpu.make_async_copy(hull_hbm, hullm, lsem.at[1]),
        pltpu.make_async_copy(surf_hbm, surf, lsem.at[2]),
        pltpu.make_async_copy(sten_hbm.at[:, :, own], sten.at[:, levels], lsem.at[3]),
        pltpu.make_async_copy(src_hbm.at[:, own], srcl.at[levels], lsem.at[4]),
        pltpu.make_async_copy(elev_hbm, elev, lsem.at[5]),
        pltpu.make_async_copy(cinv_hbm, cinv, lsem.at[6]),
    ]
    for copy in local:
        copy.start()

    pl.semaphore_wait(barrier, count)

    partner = (s, t, 1 - v)
    cross = [
        pltpu.make_async_remote_copy(
            src, dst, xs_sem.at[i], xr_sem.at[i], device_id=partner, device_id_type=MESH
        )
        for i, (src, dst) in enumerate(
            (
                (pot_hbm.at[:, other], pot.at[levels]),
                (sten_hbm.at[:, :, other], sten.at[:, levels]),
                (src_hbm.at[:, other], srcl.at[levels]),
            )
        )
    ]
    for copy in cross:
        copy.start()

    lane = lax.broadcasted_iota(jnp.int32, (8, 128), 1)
    sub = lax.broadcasted_iota(jnp.int32, (8, 128), 0)

    def row_copy(k, role):
        return pltpu.make_async_remote_copy(
            rows_s.at[k, role], rows_r.at[k, role], row_ss.at[k, role], row_rs.at[k, role],
            device_id=(role_dev[role][0], t, role_dev[role][1]), device_id_type=MESH,
        )

    def pack_copy(k, side):
        return pltpu.make_async_remote_copy(
            packs_s.at[k, side], packs_r.at[k, 1 - side], pack_ss.at[k, side], pack_rs.at[k, 1 - side],
            device_id=(s, side_t[side], v), device_id_type=MESH,
        )

    def diag_copy(k, role, side):
        return pltpu.make_async_remote_copy(
            diag_s.at[k, role], diag_r.at[k, role, pl.ds(8 * (1 - side), 8)],
            diag_ss.at[k, role, side], diag_rs.at[k, role, 1 - side],
            device_id=(role_dev[role][0], side_t[side], role_dev[role][1]), device_id_type=MESH,
        )

    def send_row(k, role, line, top_line):
        whole = jnp.concatenate(
            [
                jnp.broadcast_to(line[0:1], (8, 128)),
                line,
                jnp.broadcast_to(top_line, (8, 128)),
                jnp.zeros((48, 128), F32),
            ],
            axis=0,
        )
        rows_s[k, role] = whole[0:80]

        @pl.when(role_ok[role])
        def _():
            row_copy(k, role).start()

        turned = jnp.transpose(whole)
        diag_s[k, role] = jnp.concatenate(
            [turned[0:1], turned[127:128], jnp.zeros((6, 128), F32)], axis=0
        )
        for side in range(2):

            @pl.when(role_ok[role] & side_ok[side])
            def _():
                diag_copy(k, role, side).start()

    def send_packs(k):
        def one(z, carry):
            left, right = carry
            turned = pltpu.roll(field[pl.ds(pl.multiple_of(8 * z + 8, 8), 8), :], z, 1)
            left = jnp.where(lane == z, turned, left)
            right = jnp.where(lane == (z + 127) % 128, turned, right)
            return left, right

        zero = jnp.zeros((8, 128), F32)
        left, right = lax.fori_loop(0, 65, one, (zero, zero), unroll=5)
        packs_s[k, 0] = left
        packs_s[k, 1] = pltpu.roll(right, 1, 1)
        for side in range(2):

            @pl.when(side_ok[side])
            def _():
                pack_copy(k, side).start()

    def close_field():
        field[0:8, :] = field[8:16, :]
        field[520:528, :] = hull[...] * field[512:520, :] + top[...]

    def column(ref, x, first):
        return ref[pl.ds(x + first, 64, stride=8), :]

    local[0].wait()
    local[1].wait()
    local[2].wait()
    hull[...] = hullm[...].astype(F32)
    top[...] = (1.0 - hull[...]) * surf[...]
    cross[0].wait_recv()
    field[8:520, :] = pot[...].reshape(512, 128)
    close_field()
    for role in range(2):
        x = edge_x[role]
        send_row(0, role, column(field, x, 8), field[pl.ds(x + 520, 1), :])
    send_packs(0)

    local[5].wait()
    local[6].wait()
    weight[...] = 0.5 * (1.0 + elev[...]) * (1.0 + elev[...])
    both = cinv[...].reshape(128, 64)
    high = both.astype(BF16).astype(F32)
    lhs[...] = jnp.concatenate([high, high, both - high], axis=1).astype(BF16)
    local[4].wait()
    cross[2].wait_recv()
    applied[...] = srcl[...].reshape(512, 128)
    for x in range(8):
        resid[x] = column(applied, x, 0)
        corr[x] = jnp.zeros((64, 128), F32)
    local[3].wait()
    cross[1].wait_recv()

    def widen(o, _):
        def block(i, _):
            coef[o, pl.ds(pl.multiple_of(64 * i, 64), 64), :] = (
                sten[o, pl.ds(8 * i, 8)].astype(F32).reshape(64, 128)
            )
            return 0

        return lax.fori_loop(0, 8, block, 0, unroll=True)

    lax.fori_loop(0, 27, widen, 0)
    for role in range(2):
        for a in range(3):
            for c in range(3):
                o = 9 * a + 3 * edge_b[role] + c
                edge[role, 3 * a + c] = coef[o, pl.ds(edge_x[role], 64, stride=8), :]

    def solve(u, hull_line):
        hi = u.astype(BF16)
        lo = (u - hi.astype(F32)).astype(BF16)
        y = jnp.dot(lhs[...], jnp.concatenate([hi, lo, hi], axis=0), preferred_element_type=F32)
        return jnp.where(hull_line > 0.5, y[64:128], y[0:64])

    lane80 = lax.broadcasted_iota(jnp.int32, (80, 128), 1)

    def ghost_part(k, role):
        @pl.when(role_ok[role])
        def _():
            row_copy(k, role).wait_recv()

        for side in range(2):

            @pl.when(role_ok[role] & side_ok[side])
            def _():
                diag_copy(k, role, 1 - side).wait_recv()

        line = rows_r[k, role]
        turned = jnp.transpose(
            jnp.concatenate([diag_r[k, role], jnp.zeros((112, 128), F32)], axis=0)
        )
        ghost3[0] = jnp.where(lane80 == 0, turned[0:80, 1:2], pltpu.roll(line, 1, 1))
        ghost3[1] = line
        ghost3[2] = jnp.where(lane80 == 127, turned[0:80, 8:9], pltpu.roll(line, 127, 1))
        total = jnp.zeros((64, 128), F32)
        for a in range(3):
            for c in range(3):
                total = total + edge[role, 3 * a + c] * ghost3[c, 7 + a : 71 + a, :]
        return total

    def out_copies(i, hbm):
        mine = pltpu.make_async_copy(outl.at[i, levels], hbm.at[:, own], out_ls.at[i])
        theirs = pltpu.make_async_remote_copy(
            outl.at[i, pl.ds(32 * (1 - v), 32)], hbm.at[:, own], out_ss.at[i], out_rs.at[i],
            device_id=partner, device_id_type=MESH,
        )
        return mine, theirs

    def sweep(k, _):
        for side in range(2):

            @pl.when(side_ok[side])
            def _():
                pack_copy(k, 1 - side).wait_recv()

        from_left = packs_r[k, 0]
        from_right = packs_r[k, 1]

        def shift(z, _):
            here = pl.ds(pl.multiple_of(8 * z, 8), 8)
            level = jnp.clip(z - 1, 0, 64)
            middle = field[here, :]
            left = jnp.where(lane == 0, pltpu.roll(from_left, (128 - level) % 128, 1), pltpu.roll(middle, 1, 1))
            right = jnp.where(lane == 127, pltpu.roll(from_right, 127 - level, 1), pltpu.roll(middle, 127, 1))
            for c, value in enumerate((left, middle, right)):
                shifted[c, here, :] = jnp.where(sub == 0, 0.0, pltpu.roll(value, 1, 0))
                shifted[3 + c, here, :] = value
                shifted[6 + c, here, :] = jnp.where(sub == 7, 0.0, pltpu.roll(value, 7, 0))
            return 0

        lax.fori_loop(0, 66, shift, 0, unroll=3)

        def block(i, _):
            at = pl.multiple_of(64 * i, 64)
            total = jnp.zeros((64, 128), F32)
            for b in range(3):
                for c in range(3):
                    window = shifted[3 * b + c, pl.ds(at, 80), :]
                    for a in range(3):
                        total = total + coef[9 * a + 3 * b + c, pl.ds(at, 64), :] * window[8 * a : 8 * a + 64]
            applied[pl.ds(at, 64), :] = total
            return 0

        lax.fori_loop(0, 8, block, 0)

        part = ghost_part(k, 1)
        resid_x = edge_x[1]
        applied[pl.ds(resid_x, 64, stride=8), :] = column(applied, resid_x, 0) + part

        for pair in range(4):
            lines = []
            for x in (2 * pair, 2 * pair + 1):
                u = resid[x] - column(applied, x, 0)

                @pl.when(k == 0)
                def _():
                    resid[x] = u

                lines.append(u)
            u = jnp.concatenate(lines, axis=1)
            mask = jnp.concatenate([hull[2 * pair : 2 * pair + 1], hull[2 * pair + 1 : 2 * pair + 2]], axis=1)
            step = solve(u, mask)
            for i, x in enumerate((2 * pair, 2 * pair + 1)):
                corr[x] = corr[x] + weight[x : x + 1] * step[:, 128 * i : 128 * i + 128]

        part = ghost_part(k, 0)
        x = edge_x[0]

        @pl.when(k == 0)
        def _():
            resid[x] = resid[x] - part
            top[...] = jnp.zeros((8, 128), F32)

        line_hull = hull[pl.ds(x, 1), :]
        corr[x] = corr[x] - weight[pl.ds(x, 1), :] * solve(part, line_hull)

        @pl.when(k < SWEEPS - 1)
        def _():
            for role in range(2):
                x = edge_x[role]
                line = corr[x]
                send_row(k + 1, role, line, hull[pl.ds(x, 1), :] * line[63:64])

        for x in range(8):
            field[pl.ds(8 + x, 64, stride=8), :] = corr[x]
        close_field()

        @pl.when(k < SWEEPS - 1)
        def _():
            send_packs(k + 1)

        @pl.when(k == 0)
        def _():
            for x in range(8):
                applied[pl.ds(x, 64, stride=8), :] = resid[x]
            outl[0] = applied[...].reshape(64, 8, 128)
            for copy in out_copies(0, res_hbm):
                copy.start()

        return 0

    lax.fori_loop(0, SWEEPS, sweep, 0)

    outl[1] = pot[...] + field[8:520, :].reshape(64, 8, 128)
    for copy in out_copies(1, upd_hbm):
        copy.start()

    for copy in cross:
        copy.wait_send()

    def drain(k, _):
        for role in range(2):

            @pl.when(role_ok[role])
            def _():
                row_copy(k, role).wait_send()

            @pl.when(side_ok[role])
            def _():
                pack_copy(k, role).wait_send()

            for side in range(2):

                @pl.when(role_ok[role] & side_ok[side])
                def _():
                    diag_copy(k, role, side).wait_send()

        return 0

    lax.fori_loop(0, SWEEPS, drain, 0)
    for i, hbm in enumerate((res_hbm, upd_hbm)):
        mine, theirs = out_copies(i, hbm)
        mine.wait()
        theirs.wait_send()
        pltpu.make_async_remote_copy(
            outl.at[i, levels], hbm.at[:, other], out_ss.at[i], out_rs.at[i],
            device_id=partner, device_id_type=MESH,
        ).wait_recv()


def per_device(potential, source, stencil, surface_potential, elevation, hull_mask, column_inverse):
    vm = pltpu.VMEM
    dma = pltpu.SemaphoreType.DMA
    n = SWEEPS
    return pl.pallas_call(
        kernel,
        out_shape=(jax.ShapeDtypeStruct((32, 16, 128), F32), jax.ShapeDtypeStruct((32, 16, 128), F32)),
        in_specs=[pl.BlockSpec(memory_space=pl.ANY)] * 7,
        out_specs=(pl.BlockSpec(memory_space=pl.ANY), pl.BlockSpec(memory_space=pl.ANY)),
        scratch_shapes=[
            vm((64, 8, 128), F32), vm((64, 8, 128), F32), vm((27, 64, 8, 128), BF16), vm((8, 128), F32), vm((8, 128), F32),
            vm((8, 128), jnp.int32), vm((2, 64, 64), F32),
            vm((27, 512, 128), F32), vm((2, 9, 64, 128), F32), vm((9, 528, 128), F32), vm((528, 128), F32), vm((512, 128), F32),
            vm((8, 64, 128), F32), vm((8, 64, 128), F32), vm((8, 128), F32), vm((8, 128), F32), vm((8, 128), F32), vm((128, 192), BF16),
            vm((3, 80, 128), F32), vm((2, 64, 8, 128), F32),
            vm((n, 2, 80, 128), F32), vm((n, 2, 80, 128), F32), vm((n, 2, 8, 128), F32), vm((n, 2, 8, 128), F32),
            vm((n, 2, 8, 128), F32), vm((n, 2, 16, 128), F32),
            dma((7,)), dma((3,)), dma((3,)), dma((n, 2)), dma((n, 2)), dma((n, 2)), dma((n, 2)), dma((n, 2, 2)), dma((n, 2, 2)),
            dma((2,)), dma((2,)), dma((2,)),
        ],
        compiler_params=pltpu.CompilerParams(collective_id=0, has_side_effects=True, vmem_limit_bytes=60 * 1024 * 1024),
        name="defect_correction",
    )(potential, source, stencil, surface_potential, elevation, hull_mask, column_inverse)


def solution(mesh):
    return jax.shard_map(
        per_device,
        mesh=mesh,
        in_specs=(
            P("vert", "ship", "trans"),
            P("vert", "ship", "trans"),
            P(None, "vert", "ship", "trans"),
            P(("ship", "vert"), "trans"),
            P(("ship", "vert"), "trans"),
            P(("ship", "vert"), "trans"),
            P(),
        ),
        out_specs=(P("vert", "ship", "trans"), P("vert", "ship", "trans")),
        check_vma=False,
    )
```

```python
import jax
import jax.numpy as jnp
from jax import lax
from jax.experimental import pallas as pl
from jax.experimental.pallas import tpu as pltpu
from jax.sharding import PartitionSpec as P

SWEEPS = 4
MESH = pl.DeviceIdType.MESH
F32 = jnp.float32
BF16 = jnp.bfloat16


def kernel(
    pot_hbm, src_hbm, sten_hbm, surf_hbm, elev_hbm, hull_hbm, cinv_hbm,
    upd_hbm, res_hbm,
    pot, srcl, sten, surf, elev, hullm, cinv,
    coef, edge, shifted, field, applied, resid, corr, hull, weight, top, lhs, ghost3, outl,
    rows_s, rows_r, packs_s, packs_r, diag_s, diag_r,
    slab, line_s, prof_s, prof_r, rim_s, rim_r,
    line_ss, line_rs, prof_ss, prof_rs, rim_ss, rim_rs,
    lsem, xs_sem, xr_sem, row_ss, row_rs, pack_ss, pack_rs, diag_ss, diag_rs, out_ss, out_rs, out_ls,
):
    s = lax.axis_index("ship")
    t = lax.axis_index("trans")
    v = lax.axis_index("vert")
    ships = lax.axis_size("ship")
    transes = lax.axis_size("trans")
    slow_ok = jnp.where(v == 0, s > 0, s < ships - 1)
    role_ok = (slow_ok, s >= 0)
    role_dev = ((s + 2 * v - 1, 1 - v), (s, 1 - v))
    side_ok = (t > 0, t < transes - 1)
    side_t = (t - 1, t + 1)
    edge_x = (7 * v, 7 * (1 - v))
    edge_b = (2 * v, 2 * (1 - v))

    def clear(k, _):
        for role in range(2):
            rows_r[k, role] = jnp.zeros((80, 128), F32)
            packs_r[k, role] = jnp.zeros((8, 128), F32)
            diag_r[k, role] = jnp.zeros((16, 128), F32)
        return 0

    lax.fori_loop(0, SWEEPS, clear, 0)
    prof_r[...] = jnp.zeros_like(prof_r)
    rim_r[...] = jnp.zeros_like(rim_r)

    barrier = pltpu.get_barrier_semaphore()
    count = 0
    chip_ok = (s > 0, s < ships - 1)
    chip_s = (s - 1, s + 1)
    met = [(role_ok[role], *role_dev[role]) for role in range(2)] + [(chip_ok[i], chip_s[i], v) for i in range(2)]
    for there, ship, vert in met:
        for ok, tt in ((there, t), (there & side_ok[0], t - 1), (there & side_ok[1], t + 1)):

            @pl.when(ok)
            def _():
                pl.semaphore_signal(barrier, inc=1, device_id=(ship, tt, vert), device_id_type=MESH)

            count = count + ok.astype(jnp.int32)
    for side in range(2):

        @pl.when(side_ok[side])
        def _():
            pl.semaphore_signal(barrier, inc=1, device_id=(s, side_t[side], v), device_id_type=MESH)

        count = count + side_ok[side].astype(jnp.int32)

    own = pl.ds(pl.multiple_of(8 * v, 8), 8)
    other = pl.ds(pl.multiple_of(8 * (1 - v), 8), 8)
    levels = pl.ds(32 * v, 32)
    whole_slab = pltpu.make_async_copy(pot_hbm, slab, lsem.at[7])
    whole_slab.start()
    local = [
        pltpu.make_async_copy(pot_hbm.at[:, own], pot.at[levels], lsem.at[0]),
        pltpu.make_async_copy(hull_hbm, hullm, lsem.at[1]),
        pltpu.make_async_copy(surf_hbm, surf, lsem.at[2]),
        pltpu.make_async_copy(sten_hbm.at[:, :, own], sten.at[:, levels], lsem.at[3]),
        pltpu.make_async_copy(src_hbm.at[:, own], srcl.at[levels], lsem.at[4]),
        pltpu.make_async_copy(elev_hbm, elev, lsem.at[5]),
        pltpu.make_async_copy(cinv_hbm, cinv, lsem.at[6]),
    ]
    for copy in local:
        copy.start()

    lane = lax.broadcasted_iota(jnp.int32, (8, 128), 1)
    sub = lax.broadcasted_iota(jnp.int32, (8, 128), 0)

    def line_copy(dirn, core):
        return pltpu.make_async_remote_copy(
            line_s.at[dirn], rows_r.at[0, 0, pl.ds(pl.multiple_of(8 + 32 * core, 8), 32)],
            line_ss.at[dirn], line_rs.at[core],
            device_id=(chip_s[dirn], t, 1 - dirn), device_id_type=MESH,
        )

    def prof_copy(dirn, side, core):
        return pltpu.make_async_remote_copy(
            prof_s.at[dirn], prof_r.at[core, pl.ds(8 * (1 - side), 8)],
            prof_ss.at[dirn, side], prof_rs.at[core, 1 - side],
            device_id=(chip_s[dirn], side_t[side], 1 - dirn), device_id_type=MESH,
        )

    def rim_copy(place):
        return pltpu.make_async_remote_copy(
            rim_s, rim_r.at[(1, 0, 2)[place]], rim_ss.at[place], rim_rs.at[(1, 0, 2)[place]],
            device_id=(role_dev[0][0], (side_t + (t,))[place], role_dev[0][1]), device_id_type=MESH,
        )

    rim_ok = (slow_ok & side_ok[0], slow_ok & side_ok[1], slow_ok)
    whole_slab.wait()
    first, last = slab[:, 0, :], slab[:, 15, :]
    line_s[0] = first
    line_s[1] = last
    turned = jnp.transpose(jnp.concatenate([first, last, jnp.zeros((64, 128), F32)], axis=0))
    ends = jnp.concatenate([turned[0:1], turned[127:128], jnp.zeros((6, 128), F32)], axis=0)
    prof_s[0] = pltpu.roll(ends, 8 + 32 * v, 1)
    prof_s[1] = pltpu.roll(ends, (104 + 32 * v) % 128, 1)
    local[1].wait()
    local[2].wait()
    hull[...] = hullm[...].astype(F32)
    top[...] = (1.0 - hull[...]) * surf[...]
    rim_s[0:1] = hull[pl.ds(edge_x[0], 1), :]
    rim_s[1:2] = top[pl.ds(edge_x[0], 1), :]
    rim_s[2:8] = jnp.zeros((6, 128), F32)

    pl.semaphore_wait(barrier, count)

    for dirn in range(2):

        @pl.when(chip_ok[dirn])
        def _():
            line_copy(dirn, v).start()

        for side in range(2):

            @pl.when(chip_ok[dirn] & side_ok[side])
            def _():
                prof_copy(dirn, side, v).start()

    for place in range(3):

        @pl.when(rim_ok[place])
        def _():
            rim_copy(place).start()

    partner = (s, t, 1 - v)
    cross = [
        pltpu.make_async_remote_copy(
            src, dst, xs_sem.at[i], xr_sem.at[i], device_id=partner, device_id_type=MESH
        )
        for i, (src, dst) in enumerate(
            (
                (pot_hbm.at[:, other], pot.at[levels]),
                (sten_hbm.at[:, :, other], sten.at[:, levels]),
                (src_hbm.at[:, other], srcl.at[levels]),
            )
        )
    ]
    for copy in cross:
        copy.start()

    def row_copy(k, role):
        return pltpu.make_async_remote_copy(
            rows_s.at[k, role], rows_r.at[k, role], row_ss.at[k, role], row_rs.at[k, role],
            device_id=(role_dev[role][0], t, role_dev[role][1]), device_id_type=MESH,
        )

    def pack_copy(k, side):
        return pltpu.make_async_remote_copy(
            packs_s.at[k, side], packs_r.at[k, 1 - side], pack_ss.at[k, side], pack_rs.at[k, 1 - side],
            device_id=(s, side_t[side], v), device_id_type=MESH,
        )

    def diag_copy(k, role, side):
        return pltpu.make_async_remote_copy(
            diag_s.at[k, role], diag_r.at[k, role, pl.ds(8 * (1 - side), 8)],
            diag_ss.at[k, role, side], diag_rs.at[k, role, 1 - side],
            device_id=(role_dev[role][0], side_t[side], role_dev[role][1]), device_id_type=MESH,
        )

    def send_row(k, role, line, top_line):
        whole = jnp.concatenate(
            [
                jnp.broadcast_to(line[0:1], (8, 128)),
                line,
                jnp.broadcast_to(top_line, (8, 128)),
                jnp.zeros((48, 128), F32),
            ],
            axis=0,
        )
        rows_s[k, role] = whole[0:80]

        @pl.when(role_ok[role])
        def _():
            row_copy(k, role).start()

        turned = jnp.transpose(whole)
        diag_s[k, role] = jnp.concatenate(
            [turned[0:1], turned[127:128], jnp.zeros((6, 128), F32)], axis=0
        )
        for side in range(2):

            @pl.when(role_ok[role] & side_ok[side])
            def _():
                diag_copy(k, role, side).start()

    def send_packs(k):
        left = jnp.zeros((8, 128), F32)
        right = left
        for z in range(65):
            turned = pltpu.roll(field[8 * z + 8 : 8 * z + 16, :], z, 1)
            left = jnp.where(lane == z, turned, left)
            right = jnp.where(lane == (z + 127) % 128, turned, right)
        packs_s[k, 0] = left
        packs_s[k, 1] = pltpu.roll(right, 1, 1)
        for side in range(2):

            @pl.when(side_ok[side])
            def _():
                pack_copy(k, side).start()

    def close_field():
        field[0:8, :] = field[8:16, :]
        field[520:528, :] = hull[...] * field[512:520, :] + top[...]

    def column(ref, x, first):
        return ref[pl.ds(x + first, 64, stride=8), :]

    def widen(core):
        def one(o, _):
            for i in range(4):
                at = 32 * core + 8 * i
                coef[o, pl.ds(pl.multiple_of(8 * at, 64), 64), :] = (
                    sten[o, pl.ds(at, 8)].astype(F32).reshape(64, 128)
                )
            return 0

        lax.fori_loop(0, 27, one, 0)

    local[5].wait()
    local[6].wait()
    weight[...] = 0.5 * (1.0 + elev[...]) * (1.0 + elev[...])
    both = cinv[...].reshape(128, 64)
    high = both.astype(BF16).astype(F32)
    lhs[...] = jnp.concatenate([high, high, both - high], axis=1).astype(BF16)
    local[3].wait()
    widen(v)

    local[0].wait()
    cross[0].wait_recv()
    field[8:520, :] = pot[...].reshape(512, 128)
    close_field()
    send_row(0, 1, column(field, edge_x[1], 8), field[pl.ds(edge_x[1] + 520, 1), :])
    send_packs(0)

    local[4].wait()
    cross[2].wait_recv()
    applied[...] = srcl[...].reshape(512, 128)
    for x in range(8):
        resid[x] = column(applied, x, 0)
        corr[x] = jnp.zeros((64, 128), F32)
    cross[1].wait_recv()
    widen(1 - v)
    for role in range(2):
        for a in range(3):
            for c in range(3):
                o = 9 * a + 3 * edge_b[role] + c
                edge[role, 3 * a + c] = coef[o, pl.ds(edge_x[role], 64, stride=8), :]

    def solve(u, hull_line):
        hi = u.astype(BF16)
        lo = (u - hi.astype(F32)).astype(BF16)
        y = jnp.dot(lhs[...], jnp.concatenate([hi, lo, hi], axis=0), preferred_element_type=F32)
        return jnp.where(hull_line > 0.5, y[64:128], y[0:64])

    lane80 = lax.broadcasted_iota(jnp.int32, (80, 128), 1)

    def gather_first():
        for core in range(2):

            @pl.when(slow_ok)
            def _():
                line_copy(0, core).wait_recv()

            for side in range(2):

                @pl.when(slow_ok & side_ok[side])
                def _():
                    prof_copy(0, 1 - side, core).wait_recv()

        for place in range(3):

            @pl.when(rim_ok[place])
            def _():
                rim_copy((1, 0, 2)[place]).wait_recv()

        rows_r[0, 0, 0:8] = jnp.broadcast_to(rows_r[0, 0, 8:9], (8, 128))
        rows_r[0, 0, 72:80] = jnp.broadcast_to(
            rim_r[2, 0:1] * rows_r[0, 0, 71:72] + rim_r[2, 1:2], (8, 128)
        )
        for side in range(2):
            part = pl.ds(8 * side, 8)
            level = jnp.where(lane < 40, prof_r[0, part], prof_r[1, part])
            level = jnp.where(lane == 7, pltpu.roll(level, 127, 1), level)
            turn = (73, 72)[side]
            rim_hull = pltpu.roll(jnp.broadcast_to(rim_r[side, 0:1], (8, 128)), turn, 1)
            rim_top = pltpu.roll(jnp.broadcast_to(rim_r[side, 1:2], (8, 128)), turn, 1)
            diag_r[0, 0, part] = jnp.where(lane == 72, rim_hull * pltpu.roll(level, 1, 1) + rim_top, level)

    def ghost_part(k, role):
        here = role_ok[role] & (k > 0) if role == 0 else role_ok[role]

        @pl.when(here)
        def _():
            row_copy(k, role).wait_recv()

        for side in range(2):

            @pl.when(here & side_ok[side])
            def _():
                diag_copy(k, role, 1 - side).wait_recv()

        if role == 0:

            @pl.when(k == 0)
            def _():
                gather_first()

        line = rows_r[k, role]
        turned = jnp.transpose(
            jnp.concatenate([diag_r[k, role], jnp.zeros((112, 128), F32)], axis=0)
        )
        ghost3[0] = jnp.where(lane80 == 0, turned[0:80, 1:2], pltpu.roll(line, 1, 1))
        ghost3[1] = line
        ghost3[2] = jnp.where(lane80 == 127, turned[0:80, 8:9], pltpu.roll(line, 127, 1))
        total = jnp.zeros((64, 128), F32)
        for a in range(3):
            for c in range(3):
                total = total + edge[role, 3 * a + c] * ghost3[c, 7 + a : 71 + a, :]
        return total

    def out_copies(i, hbm):
        mine = pltpu.make_async_copy(outl.at[i, levels], hbm.at[:, own], out_ls.at[i])
        theirs = pltpu.make_async_remote_copy(
            outl.at[i, pl.ds(32 * (1 - v), 32)], hbm.at[:, own], out_ss.at[i], out_rs.at[i],
            device_id=partner, device_id_type=MESH,
        )
        return mine, theirs

    def sweep(k, _):
        for side in range(2):

            @pl.when(side_ok[side])
            def _():
                pack_copy(k, 1 - side).wait_recv()

        from_left = packs_r[k, 0]
        from_right = packs_r[k, 1]

        def shift(z, _):
            here = pl.ds(pl.multiple_of(8 * z, 8), 8)
            level = jnp.clip(z - 1, 0, 64)
            middle = field[here, :]
            left = jnp.where(lane == 0, pltpu.roll(from_left, (128 - level) % 128, 1), pltpu.roll(middle, 1, 1))
            right = jnp.where(lane == 127, pltpu.roll(from_right, 127 - level, 1), pltpu.roll(middle, 127, 1))
            for c, value in enumerate((left, middle, right)):
                shifted[c, here, :] = jnp.where(sub == 0, 0.0, pltpu.roll(value, 1, 0))
                shifted[3 + c, here, :] = value
                shifted[6 + c, here, :] = jnp.where(sub == 7, 0.0, pltpu.roll(value, 7, 0))
            return 0

        lax.fori_loop(0, 66, shift, 0, unroll=11)

        def block(i, _):
            at = pl.multiple_of(64 * i, 64)
            total = jnp.zeros((64, 128), F32)
            for b in range(3):
                for c in range(3):
                    window = shifted[3 * b + c, pl.ds(at, 80), :]
                    for a in range(3):
                        total = total + coef[9 * a + 3 * b + c, pl.ds(at, 64), :] * window[8 * a : 8 * a + 64]
            applied[pl.ds(at, 64), :] = total
            return 0

        lax.fori_loop(0, 8, block, 0)

        part = ghost_part(k, 1)
        resid_x = edge_x[1]
        applied[pl.ds(resid_x, 64, stride=8), :] = column(applied, resid_x, 0) + part

        for pair in range(4):
            lines = []
            for x in (2 * pair, 2 * pair + 1):
                u = resid[x] - column(applied, x, 0)

                @pl.when(k == 0)
                def _():
                    resid[x] = u

                lines.append(u)
            u = jnp.concatenate(lines, axis=1)
            mask = jnp.concatenate([hull[2 * pair : 2 * pair + 1], hull[2 * pair + 1 : 2 * pair + 2]], axis=1)
            step = solve(u, mask)
            for i, x in enumerate((2 * pair, 2 * pair + 1)):
                corr[x] = corr[x] + weight[x : x + 1] * step[:, 128 * i : 128 * i + 128]

        part = ghost_part(k, 0)
        x = edge_x[0]

        @pl.when(k == 0)
        def _():
            resid[x] = resid[x] - part
            top[...] = jnp.zeros((8, 128), F32)

        line_hull = hull[pl.ds(x, 1), :]
        corr[x] = corr[x] - weight[pl.ds(x, 1), :] * solve(part, line_hull)

        @pl.when(k < SWEEPS - 1)
        def _():
            for role in range(2):
                x = edge_x[role]
                line = corr[x]
                send_row(k + 1, role, line, hull[pl.ds(x, 1), :] * line[63:64])

        for x in range(8):
            field[pl.ds(8 + x, 64, stride=8), :] = corr[x]
        close_field()

        @pl.when(k < SWEEPS - 1)
        def _():
            send_packs(k + 1)

        @pl.when(k == 0)
        def _():
            for x in range(8):
                applied[pl.ds(x, 64, stride=8), :] = resid[x]
            outl[0] = applied[...].reshape(64, 8, 128)
            for copy in out_copies(0, res_hbm):
                copy.start()

        return 0

    lax.fori_loop(0, SWEEPS, sweep, 0)

    outl[1] = pot[...] + field[8:520, :].reshape(64, 8, 128)
    for copy in out_copies(1, upd_hbm):
        copy.start()

    for copy in cross:
        copy.wait_send()

    def drain(k, _):
        for role in range(2):
            sent = role_ok[role] & (k > 0) if role == 0 else role_ok[role]

            @pl.when(sent)
            def _():
                row_copy(k, role).wait_send()

            @pl.when(side_ok[role])
            def _():
                pack_copy(k, role).wait_send()

            for side in range(2):

                @pl.when(sent & side_ok[side])
                def _():
                    diag_copy(k, role, side).wait_send()

        return 0

    lax.fori_loop(0, SWEEPS, drain, 0)
    for dirn in range(2):

        @pl.when(chip_ok[dirn])
        def _():
            line_copy(dirn, v).wait_send()

        for side in range(2):

            @pl.when(chip_ok[dirn] & side_ok[side])
            def _():
                prof_copy(dirn, side, v).wait_send()

    for place in range(3):

        @pl.when(rim_ok[place])
        def _():
            rim_copy(place).wait_send()

    for i, hbm in enumerate((res_hbm, upd_hbm)):
        mine, theirs = out_copies(i, hbm)
        mine.wait()
        theirs.wait_send()
        pltpu.make_async_remote_copy(
            outl.at[i, levels], hbm.at[:, other], out_ss.at[i], out_rs.at[i],
            device_id=partner, device_id_type=MESH,
        ).wait_recv()


def store(upd_vmem, res_vmem, upd_hbm, res_hbm, sem):
    copies = [
        pltpu.make_async_copy(upd_vmem, upd_hbm, sem.at[0]),
        pltpu.make_async_copy(res_vmem, res_hbm, sem.at[1]),
    ]
    for copy in copies:
        copy.start()
    for copy in copies:
        copy.wait()


def per_device(potential, source, stencil, surface_potential, elevation, hull_mask, column_inverse):
    vm = pltpu.VMEM
    dma = pltpu.SemaphoreType.DMA
    n = SWEEPS
    held = pl.pallas_call(
        kernel,
        out_shape=(vm((32, 16, 128), F32), vm((32, 16, 128), F32)),
        in_specs=[pl.BlockSpec(memory_space=pl.ANY)] * 7,
        out_specs=(pl.BlockSpec(memory_space=pl.ANY), pl.BlockSpec(memory_space=pl.ANY)),
        scratch_shapes=[
            vm((64, 8, 128), F32), vm((64, 8, 128), F32), vm((27, 64, 8, 128), BF16), vm((8, 128), F32), vm((8, 128), F32),
            vm((8, 128), jnp.int32), vm((2, 64, 64), F32),
            vm((27, 512, 128), F32), vm((2, 9, 64, 128), F32), vm((9, 528, 128), F32), vm((528, 128), F32), vm((512, 128), F32),
            vm((8, 64, 128), F32), vm((8, 64, 128), F32), vm((8, 128), F32), vm((8, 128), F32), vm((8, 128), F32), vm((128, 192), BF16),
            vm((3, 80, 128), F32), vm((2, 64, 8, 128), F32),
            vm((n, 2, 80, 128), F32), vm((n, 2, 80, 128), F32), vm((n, 2, 8, 128), F32), vm((n, 2, 8, 128), F32),
            vm((n, 2, 8, 128), F32), vm((n, 2, 16, 128), F32),
            vm((32, 16, 128), F32), vm((2, 32, 128), F32), vm((2, 8, 128), F32), vm((2, 16, 128), F32), vm((8, 128), F32), vm((3, 8, 128), F32),
            dma((2,)), dma((2,)), dma((2, 2)), dma((2, 2)), dma((3,)), dma((3,)),
            dma((8,)), dma((3,)), dma((3,)), dma((n, 2)), dma((n, 2)), dma((n, 2)), dma((n, 2)), dma((n, 2, 2)), dma((n, 2, 2)),
            dma((2,)), dma((2,)), dma((2,)),
        ],
        compiler_params=pltpu.CompilerParams(collective_id=0, has_side_effects=True, vmem_limit_bytes=60 * 1024 * 1024),
        name="defect_correction",
    )(potential, source, stencil, surface_potential, elevation, hull_mask, column_inverse)
    return pl.pallas_call(
        store,
        out_shape=(jax.ShapeDtypeStruct((32, 16, 128), F32), jax.ShapeDtypeStruct((32, 16, 128), F32)),
        in_specs=[pl.BlockSpec(memory_space=pltpu.VMEM)] * 2,
        out_specs=(pl.BlockSpec(memory_space=pl.ANY), pl.BlockSpec(memory_space=pl.ANY)),
        scratch_shapes=[dma((2,))],
        name="store",
    )(*[pltpu.with_memory_space_constraint(x, pltpu.VMEM) for x in held])


def solution(mesh):
    return jax.shard_map(
        per_device,
        mesh=mesh,
        in_specs=(
            P("vert", "ship", "trans"),
            P("vert", "ship", "trans"),
            P(None, "vert", "ship", "trans"),
            P(("ship", "vert"), "trans"),
            P(("ship", "vert"), "trans"),
            P(("ship", "vert"), "trans"),
            P(),
        ),
        out_specs=(P("vert", "ship", "trans"), P("vert", "ship", "trans")),
        check_vma=False,
    )
```

```python
import jax
import jax.numpy as jnp
from jax import lax
from jax.experimental import pallas as pl
from jax.experimental.pallas import tpu as pltpu
from jax.sharding import PartitionSpec as P

SWEEPS = 4
MESH = pl.DeviceIdType.MESH
F32 = jnp.float32
BF16 = jnp.bfloat16


def kernel(
    pot_hbm, src_hbm, sten_hbm, surf_hbm, elev_hbm, hull_hbm, cinv_hbm,
    upd_hbm, res_hbm,
    pot, srcl, sten, surf, elev, hullm, cinv,
    coef, edge, shifted, field, applied, resid, corr, hull, weight, top, lhs, ghost3, outl,
    far_s, far_r, far_sent, far_got, first_r, near_s, near_r, packs_s, packs_r, diag_s, diag_r,
    slab, line_s, prof_s, prof_r, rim_s, rim_r,
    line_ss, line_rs, prof_ss, prof_rs, rim_ss, rim_rs,
    lsem, xs_sem, xr_sem, row_ss, row_rs, pack_ss, pack_rs, diag_ss, diag_rs, out_ss, out_rs, out_ls,
):
    s = lax.axis_index("ship")
    t = lax.axis_index("trans")
    v = lax.axis_index("vert")
    ships = lax.axis_size("ship")
    transes = lax.axis_size("trans")
    slow_ok = jnp.where(v == 0, s > 0, s < ships - 1)
    role_ok = (slow_ok, s >= 0)
    role_dev = ((s + 2 * v - 1, 1 - v), (s, 1 - v))
    side_ok = (t > 0, t < transes - 1)
    side_t = (t - 1, t + 1)
    edge_x = (7 * v, 7 * (1 - v))
    edge_b = (2 * v, 2 * (1 - v))

    barrier = pltpu.get_barrier_semaphore()
    count = 0
    chip_ok = (s > 0, s < ships - 1)
    chip_s = (s - 1, s + 1)
    met = [(role_ok[role], *role_dev[role]) for role in range(2)] + [(chip_ok[i], chip_s[i], v) for i in range(2)]
    for there, ship, vert in met:
        for ok, tt in ((there, t), (there & side_ok[0], t - 1), (there & side_ok[1], t + 1)):

            @pl.when(ok)
            def _():
                pl.semaphore_signal(barrier, inc=1, device_id=(ship, tt, vert), device_id_type=MESH)

            count = count + ok.astype(jnp.int32)
    for side in range(2):

        @pl.when(side_ok[side])
        def _():
            pl.semaphore_signal(barrier, inc=1, device_id=(s, side_t[side], v), device_id_type=MESH)

        count = count + side_ok[side].astype(jnp.int32)

    @pl.when(jnp.logical_not(slow_ok))
    def _():
        far_r[...] = jnp.zeros_like(far_r)
        first_r[...] = jnp.zeros_like(first_r)
        rim_r[2] = jnp.zeros((2, 1, 128), F32)

    for side in range(2):

        @pl.when(jnp.logical_not(side_ok[side]))
        def _():
            for k in range(SWEEPS):
                packs_r[k, side] = jnp.zeros((8, 128), F32)
                diag_r[k, 1, side] = jnp.zeros((1, 128), F32)

        @pl.when(jnp.logical_not(slow_ok & side_ok[side]))
        def _():
            rim_r[side] = jnp.zeros((2, 1, 128), F32)
            for core in range(2):
                prof_r[core, side] = jnp.zeros((1, 128), F32)
            for k in range(SWEEPS):
                diag_r[k, 0, side] = jnp.zeros((1, 128), F32)

    own = pl.ds(pl.multiple_of(8 * v, 8), 8)
    other = pl.ds(pl.multiple_of(8 * (1 - v), 8), 8)
    levels = pl.ds(32 * v, 32)
    whole_slab = pltpu.make_async_copy(pot_hbm, slab, lsem.at[7])
    whole_slab.start()
    local = [
        pltpu.make_async_copy(pot_hbm.at[:, own], pot.at[levels], lsem.at[0]),
        pltpu.make_async_copy(hull_hbm, hullm, lsem.at[1]),
        pltpu.make_async_copy(surf_hbm, surf, lsem.at[2]),
        pltpu.make_async_copy(sten_hbm.at[:, :, own], sten.at[:, levels], lsem.at[3]),
        pltpu.make_async_copy(src_hbm.at[:, own], srcl.at[levels], lsem.at[4]),
        pltpu.make_async_copy(elev_hbm, elev, lsem.at[5]),
        pltpu.make_async_copy(cinv_hbm, cinv, lsem.at[6]),
    ]
    for copy in local:
        copy.start()

    lane = lax.broadcasted_iota(jnp.int32, (8, 128), 1)
    sub = lax.broadcasted_iota(jnp.int32, (8, 128), 0)

    def line_copy(dirn, core):
        return pltpu.make_async_remote_copy(
            line_s.at[dirn], first_r.at[pl.ds(pl.multiple_of(32 * core, 32), 32)],
            line_ss.at[dirn], line_rs.at[core],
            device_id=(chip_s[dirn], t, 1 - dirn), device_id_type=MESH,
        )

    def prof_copy(dirn, side, core):
        return pltpu.make_async_remote_copy(
            prof_s.at[dirn, side], prof_r.at[core, 1 - side],
            prof_ss.at[dirn, side], prof_rs.at[core, 1 - side],
            device_id=(chip_s[dirn], side_t[side], 1 - dirn), device_id_type=MESH,
        )

    def rim_copy(place):
        return pltpu.make_async_remote_copy(
            rim_s, rim_r.at[(1, 0, 2)[place]], rim_ss.at[place], rim_rs.at[(1, 0, 2)[place]],
            device_id=(role_dev[0][0], (side_t + (t,))[place], role_dev[0][1]), device_id_type=MESH,
        )

    rim_ok = (slow_ok & side_ok[0], slow_ok & side_ok[1], slow_ok)
    whole_slab.wait()
    first, last = slab[:, 0, :], slab[:, 15, :]
    line_s[0] = first
    line_s[1] = last
    turned = jnp.transpose(jnp.concatenate([first, last, jnp.zeros((64, 128), F32)], axis=0))
    for end, at in enumerate((0, 127)):
        profile = turned[at : at + 1]
        prof_s[0, end] = pltpu.roll(profile, 8 + 32 * v, 1)
        prof_s[1, end] = pltpu.roll(profile, (104 + 32 * v) % 128, 1)
    local[1].wait()
    local[2].wait()
    hull[...] = hullm[...].astype(F32)
    top[...] = (1.0 - hull[...]) * surf[...]
    rim_s[0] = hull[pl.ds(edge_x[0], 1), :]
    rim_s[1] = top[pl.ds(edge_x[0], 1), :]

    pl.semaphore_wait(barrier, count)

    for dirn in range(2):

        @pl.when(chip_ok[dirn])
        def _():
            line_copy(dirn, v).start()

        for side in range(2):

            @pl.when(chip_ok[dirn] & side_ok[side])
            def _():
                prof_copy(dirn, side, v).start()

    for place in range(3):

        @pl.when(rim_ok[place])
        def _():
            rim_copy(place).start()

    partner = (s, t, 1 - v)
    cross = [
        pltpu.make_async_remote_copy(
            src, dst, xs_sem.at[i], xr_sem.at[i], device_id=partner, device_id_type=MESH
        )
        for i, (src, dst) in enumerate(
            (
                (pot_hbm.at[:, other], pot.at[levels]),
                (sten_hbm.at[:, :, other], sten.at[:, levels]),
                (src_hbm.at[:, other], srcl.at[levels]),
            )
        )
    ]
    for copy in cross:
        copy.start()

    def row_copy(k, role):
        src, dst = ((far_s.at[k], far_r.at[k]), (near_s.at[k], near_r.at[k]))[role]
        return pltpu.make_async_remote_copy(
            src, dst, row_ss.at[k, role], row_rs.at[k, role],
            device_id=(role_dev[role][0], t, role_dev[role][1]), device_id_type=MESH,
        )

    def pack_copy(k, side):
        return pltpu.make_async_remote_copy(
            packs_s.at[k, side], packs_r.at[k, 1 - side], pack_ss.at[k, side], pack_rs.at[k, 1 - side],
            device_id=(s, side_t[side], v), device_id_type=MESH,
        )

    def diag_copy(k, role, side):
        return pltpu.make_async_remote_copy(
            diag_s.at[k, role, side], diag_r.at[k, role, 1 - side],
            diag_ss.at[k, role, side], diag_rs.at[k, role, 1 - side],
            device_id=(role_dev[role][0], side_t[side], role_dev[role][1]), device_id_type=MESH,
        )

    def send_row(k, role, line, top_line):
        whole = jnp.concatenate(
            [
                jnp.broadcast_to(line[0:1], (8, 128)),
                line,
                jnp.broadcast_to(top_line, (8, 128)),
                jnp.zeros((48, 128), F32),
            ],
            axis=0,
        )
        if role == 0:
            sent = (line - far_sent[...]).astype(BF16)
            far_s[k] = sent
            far_sent[...] = far_sent[...] + sent.astype(F32)
        else:
            near_s[k] = whole[8:80]

        @pl.when(role_ok[role])
        def _():
            row_copy(k, role).start()

        turned = jnp.transpose(whole)
        diag_s[k, role, 0] = turned[0:1]
        diag_s[k, role, 1] = turned[127:128]
        for side in range(2):

            @pl.when(role_ok[role] & side_ok[side])
            def _():
                diag_copy(k, role, side).start()

    def send_packs(k):
        left = jnp.zeros((8, 128), F32)
        right = left
        for z in range(65):
            turned = pltpu.roll(field[8 * z + 8 : 8 * z + 16, :], z, 1)
            left = jnp.where(lane == z, turned, left)
            right = jnp.where(lane == (z + 127) % 128, turned, right)
        packs_s[k, 0] = left
        packs_s[k, 1] = pltpu.roll(right, 1, 1)
        for side in range(2):

            @pl.when(side_ok[side])
            def _():
                pack_copy(k, side).start()

    def close_field():
        field[0:8, :] = field[8:16, :]
        field[520:528, :] = hull[...] * field[512:520, :] + top[...]

    def column(ref, x, first):
        return ref[pl.ds(x + first, 64, stride=8), :]

    def widen(core):
        def one(o, _):
            for i in range(4):
                at = 32 * core + 8 * i
                coef[o, pl.ds(pl.multiple_of(8 * at, 64), 64), :] = (
                    sten[o, pl.ds(at, 8)].astype(F32).reshape(64, 128)
                )
            return 0

        lax.fori_loop(0, 27, one, 0)

    far_sent[...] = jnp.zeros((64, 128), F32)
    far_got[...] = jnp.zeros((64, 128), F32)

    local[5].wait()
    local[6].wait()
    weight[...] = 0.5 * (1.0 + elev[...]) * (1.0 + elev[...])
    both = cinv[...].reshape(128, 64)
    high = both.astype(BF16).astype(F32)
    lhs[...] = jnp.concatenate([high, high, both - high], axis=1).astype(BF16)
    local[3].wait()
    widen(v)

    local[0].wait()
    cross[0].wait_recv()
    field[8:520, :] = pot[...].reshape(512, 128)
    close_field()
    send_row(0, 1, column(field, edge_x[1], 8), field[pl.ds(edge_x[1] + 520, 1), :])
    send_packs(0)

    local[4].wait()
    cross[2].wait_recv()
    applied[...] = srcl[...].reshape(512, 128)
    for x in range(8):
        resid[x] = column(applied, x, 0)
        corr[x] = jnp.zeros((64, 128), F32)
    cross[1].wait_recv()
    widen(1 - v)
    for role in range(2):
        for a in range(3):
            for c in range(3):
                o = 9 * a + 3 * edge_b[role] + c
                edge[role, 3 * a + c] = coef[o, pl.ds(edge_x[role], 64, stride=8), :]

    def solve(u, hull_line):
        hi = u.astype(BF16)
        lo = (u - hi.astype(F32)).astype(BF16)
        y = jnp.dot(lhs[...], jnp.concatenate([hi, lo, hi], axis=0), preferred_element_type=F32)
        return jnp.where(hull_line > 0.5, y[64:128], y[0:64])

    lane80 = lax.broadcasted_iota(jnp.int32, (80, 128), 1)

    def gather_first():
        for core in range(2):

            @pl.when(slow_ok)
            def _():
                line_copy(0, core).wait_recv()

            for side in range(2):

                @pl.when(slow_ok & side_ok[side])
                def _():
                    prof_copy(0, 1 - side, core).wait_recv()

        for place in range(3):

            @pl.when(rim_ok[place])
            def _():
                rim_copy((1, 0, 2)[place]).wait_recv()

        for side in range(2):
            level = jnp.where(lane[0:1] < 40, prof_r[0, side], prof_r[1, side])
            level = jnp.where(lane[0:1] == 7, pltpu.roll(level, 127, 1), level)
            turn = (73, 72)[side]
            rim_hull = pltpu.roll(rim_r[side, 0], turn, 1)
            rim_top = pltpu.roll(rim_r[side, 1], turn, 1)
            diag_r[0, 0, side] = jnp.where(lane[0:1] == 72, rim_hull * pltpu.roll(level, 1, 1) + rim_top, level)
        ghost3[1, 8:72, :] = first_r[...]
        ghost3[1, 72:80, :] = jnp.broadcast_to(rim_r[2, 0] * first_r[63:64, :] + rim_r[2, 1], (8, 128))

    def ghost_part(k, role):
        here = role_ok[role] & (k > 0) if role == 0 else role_ok[role]

        @pl.when(here)
        def _():
            row_copy(k, role).wait_recv()

        for side in range(2):

            @pl.when(here & side_ok[side])
            def _():
                diag_copy(k, role, 1 - side).wait_recv()

        if role == 0:

            @pl.when(k == 0)
            def _():
                gather_first()

            @pl.when(k > 0)
            def _():
                line = far_got[...] + far_r[k].astype(F32)
                far_got[...] = line
                ghost3[1, 8:72, :] = line
                ghost3[1, 72:80, :] = jnp.broadcast_to(rim_r[2, 0] * line[63:64], (8, 128))

        else:
            ghost3[1, 8:80, :] = near_r[k]
        ghost3[1, 0:8, :] = jnp.broadcast_to(ghost3[1, 8:9, :], (8, 128))
        line = ghost3[1]
        turned = jnp.transpose(
            jnp.concatenate([diag_r[k, role, 0], diag_r[k, role, 1], jnp.zeros((126, 128), F32)], axis=0)
        )
        ghost3[0] = jnp.where(lane80 == 0, turned[0:80, 0:1], pltpu.roll(line, 1, 1))
        ghost3[2] = jnp.where(lane80 == 127, turned[0:80, 1:2], pltpu.roll(line, 127, 1))
        total = jnp.zeros((64, 128), F32)
        for a in range(3):
            for c in range(3):
                total = total + edge[role, 3 * a + c] * ghost3[c, 7 + a : 71 + a, :]
        return total

    def out_copies(i, hbm):
        mine = pltpu.make_async_copy(outl.at[i, levels], hbm.at[:, own], out_ls.at[i])
        theirs = pltpu.make_async_remote_copy(
            outl.at[i, pl.ds(32 * (1 - v), 32)], hbm.at[:, own], out_ss.at[i], out_rs.at[i],
            device_id=partner, device_id_type=MESH,
        )
        return mine, theirs

    def sweep(k, _):
        for side in range(2):

            @pl.when(side_ok[side])
            def _():
                pack_copy(k, 1 - side).wait_recv()

        from_left = packs_r[k, 0]
        from_right = packs_r[k, 1]

        def shift(z, _):
            here = pl.ds(pl.multiple_of(8 * z, 8), 8)
            level = jnp.clip(z - 1, 0, 64)
            middle = field[here, :]
            left = jnp.where(lane == 0, pltpu.roll(from_left, (128 - level) % 128, 1), pltpu.roll(middle, 1, 1))
            right = jnp.where(lane == 127, pltpu.roll(from_right, 127 - level, 1), pltpu.roll(middle, 127, 1))
            for c, value in enumerate((left, middle, right)):
                shifted[c, here, :] = jnp.where(sub == 0, 0.0, pltpu.roll(value, 1, 0))
                shifted[3 + c, here, :] = value
                shifted[6 + c, here, :] = jnp.where(sub == 7, 0.0, pltpu.roll(value, 7, 0))
            return 0

        lax.fori_loop(0, 66, shift, 0, unroll=11)

        def block(i, _):
            at = pl.multiple_of(64 * i, 64)
            total = jnp.zeros((64, 128), F32)
            for b in range(3):
                for c in range(3):
                    window = shifted[3 * b + c, pl.ds(at, 80), :]
                    for a in range(3):
                        total = total + coef[9 * a + 3 * b + c, pl.ds(at, 64), :] * window[8 * a : 8 * a + 64]
            applied[pl.ds(at, 64), :] = total
            return 0

        lax.fori_loop(0, 8, block, 0)

        part = ghost_part(k, 1)
        resid_x = edge_x[1]
        applied[pl.ds(resid_x, 64, stride=8), :] = column(applied, resid_x, 0) + part

        for pair in range(4):
            lines = []
            for x in (2 * pair, 2 * pair + 1):
                u = resid[x] - column(applied, x, 0)

                @pl.when(k == 0)
                def _():
                    resid[x] = u

                lines.append(u)
            u = jnp.concatenate(lines, axis=1)
            mask = jnp.concatenate([hull[2 * pair : 2 * pair + 1], hull[2 * pair + 1 : 2 * pair + 2]], axis=1)
            step = solve(u, mask)
            for i, x in enumerate((2 * pair, 2 * pair + 1)):
                corr[x] = corr[x] + weight[x : x + 1] * step[:, 128 * i : 128 * i + 128]

        @pl.when(k < SWEEPS - 1)
        def _():
            line = corr[edge_x[1]]
            send_row(k + 1, 1, line, hull[pl.ds(edge_x[1], 1), :] * line[63:64])

        part = ghost_part(k, 0)
        x = edge_x[0]

        @pl.when(k == 0)
        def _():
            resid[x] = resid[x] - part
            top[...] = jnp.zeros((8, 128), F32)

        line_hull = hull[pl.ds(x, 1), :]
        line = corr[x] - weight[pl.ds(x, 1), :] * solve(part, line_hull)
        corr[x] = line

        @pl.when(k < SWEEPS - 1)
        def _():
            send_row(k + 1, 0, line, line_hull * line[63:64])

        for x in range(8):
            field[pl.ds(8 + x, 64, stride=8), :] = corr[x]
        close_field()

        @pl.when(k < SWEEPS - 1)
        def _():
            send_packs(k + 1)

        @pl.when(k == 0)
        def _():
            for x in range(8):
                applied[pl.ds(x, 64, stride=8), :] = resid[x]
            outl[0] = applied[...].reshape(64, 8, 128)
            for copy in out_copies(0, res_hbm):
                copy.start()

        return 0

    lax.fori_loop(0, SWEEPS, sweep, 0)

    outl[1] = pot[...] + field[8:520, :].reshape(64, 8, 128)
    for copy in out_copies(1, upd_hbm):
        copy.start()

    for copy in cross:
        copy.wait_send()

    def drain(k, _):
        for role in range(2):
            sent = role_ok[role] & (k > 0) if role == 0 else role_ok[role]

            @pl.when(sent)
            def _():
                row_copy(k, role).wait_send()

            @pl.when(side_ok[role])
            def _():
                pack_copy(k, role).wait_send()

            for side in range(2):

                @pl.when(sent & side_ok[side])
                def _():
                    diag_copy(k, role, side).wait_send()

        return 0

    lax.fori_loop(0, SWEEPS, drain, 0)
    for dirn in range(2):

        @pl.when(chip_ok[dirn])
        def _():
            line_copy(dirn, v).wait_send()

        for side in range(2):

            @pl.when(chip_ok[dirn] & side_ok[side])
            def _():
                prof_copy(dirn, side, v).wait_send()

    for place in range(3):

        @pl.when(rim_ok[place])
        def _():
            rim_copy(place).wait_send()

    for i, hbm in enumerate((res_hbm, upd_hbm)):
        mine, theirs = out_copies(i, hbm)
        mine.wait()
        theirs.wait_send()
        pltpu.make_async_remote_copy(
            outl.at[i, levels], hbm.at[:, other], out_ss.at[i], out_rs.at[i],
            device_id=partner, device_id_type=MESH,
        ).wait_recv()


def store(upd_vmem, res_vmem, upd_hbm, res_hbm, sem):
    copies = [
        pltpu.make_async_copy(upd_vmem, upd_hbm, sem.at[0]),
        pltpu.make_async_copy(res_vmem, res_hbm, sem.at[1]),
    ]
    for copy in copies:
        copy.start()
    for copy in copies:
        copy.wait()


def per_device(potential, source, stencil, surface_potential, elevation, hull_mask, column_inverse):
    vm = pltpu.VMEM
    dma = pltpu.SemaphoreType.DMA
    n = SWEEPS
    held = pl.pallas_call(
        kernel,
        out_shape=(vm((32, 16, 128), F32), vm((32, 16, 128), F32)),
        in_specs=[pl.BlockSpec(memory_space=pl.ANY)] * 7,
        out_specs=(pl.BlockSpec(memory_space=pl.ANY), pl.BlockSpec(memory_space=pl.ANY)),
        scratch_shapes=[
            vm((64, 8, 128), F32), vm((64, 8, 128), F32), vm((27, 64, 8, 128), BF16), vm((8, 128), F32), vm((8, 128), F32),
            vm((8, 128), jnp.int32), vm((2, 64, 64), F32),
            vm((27, 512, 128), F32), vm((2, 9, 64, 128), F32), vm((9, 528, 128), F32), vm((528, 128), F32), vm((512, 128), F32),
            vm((8, 64, 128), F32), vm((8, 64, 128), F32), vm((8, 128), F32), vm((8, 128), F32), vm((8, 128), F32), vm((128, 192), BF16),
            vm((3, 80, 128), F32), vm((2, 64, 8, 128), F32),
            vm((n, 64, 128), BF16), vm((n, 64, 128), BF16), vm((64, 128), F32), vm((64, 128), F32), vm((64, 128), F32), vm((n, 72, 128), F32), vm((n, 72, 128), F32),
            vm((n, 2, 8, 128), F32), vm((n, 2, 8, 128), F32), vm((n, 2, 2, 1, 128), F32), vm((n, 2, 2, 1, 128), F32),
            vm((32, 16, 128), F32), vm((2, 32, 128), F32), vm((2, 2, 1, 128), F32), vm((2, 2, 1, 128), F32), vm((2, 1, 128), F32),
            vm((3, 2, 1, 128), F32),
            dma((2,)), dma((2,)), dma((2, 2)), dma((2, 2)), dma((3,)), dma((3,)),
            dma((8,)), dma((3,)), dma((3,)), dma((n, 2)), dma((n, 2)), dma((n, 2)), dma((n, 2)), dma((n, 2, 2)), dma((n, 2, 2)),
            dma((2,)), dma((2,)), dma((2,)),
        ],
        compiler_params=pltpu.CompilerParams(collective_id=0, has_side_effects=True, vmem_limit_bytes=60 * 1024 * 1024),
        name="defect_correction",
    )(potential, source, stencil, surface_potential, elevation, hull_mask, column_inverse)
    return pl.pallas_call(
        store,
        out_shape=(jax.ShapeDtypeStruct((32, 16, 128), F32), jax.ShapeDtypeStruct((32, 16, 128), F32)),
        in_specs=[pl.BlockSpec(memory_space=pltpu.VMEM)] * 2,
        out_specs=(pl.BlockSpec(memory_space=pl.ANY), pl.BlockSpec(memory_space=pl.ANY)),
        scratch_shapes=[dma((2,))],
        name="store",
    )(*[pltpu.with_memory_space_constraint(x, pltpu.VMEM) for x in held])


def solution(mesh):
    return jax.shard_map(
        per_device,
        mesh=mesh,
        in_specs=(
            P("vert", "ship", "trans"),
            P("vert", "ship", "trans"),
            P(None, "vert", "ship", "trans"),
            P(("ship", "vert"), "trans"),
            P(("ship", "vert"), "trans"),
            P(("ship", "vert"), "trans"),
            P(),
        ),
        out_specs=(P("vert", "ship", "trans"), P("vert", "ship", "trans")),
        check_vma=False,
    )
```

```python
import jax
import jax.numpy as jnp
from jax import lax
from jax.experimental import pallas as pl
from jax.experimental.pallas import tpu as pltpu
from jax.sharding import PartitionSpec as P

SWEEPS = 4
MESH = pl.DeviceIdType.MESH
F32 = jnp.float32
BF16 = jnp.bfloat16


def kernel(
    pot_hbm, src_hbm, sten_hbm, surf_hbm, elev_hbm, hull_hbm, cinv_hbm,
    upd_hbm, res_hbm,
    pot, srcl, sten, surf, elev, hullm, cinv,
    coef, edge, shifted, field, applied, resid, corr, hull, weight, top, lhs, ghost3, outl,
    far_s, far_r, far_sent, far_got, first_r, near_s, near_r, packs_s, packs_r, diag_s, diag_r,
    tail, tail_r, slab, line_s, prof_s, prof_r, rim_s, rim_r,
    tail_ss, tail_rs, line_ss, line_rs, prof_ss, prof_rs, rim_ss, rim_rs,
    lsem, xs_sem, xr_sem, row_ss, row_rs, pack_ss, pack_rs, diag_ss, diag_rs, out_ss, out_rs, out_ls,
):
    s = lax.axis_index("ship")
    t = lax.axis_index("trans")
    v = lax.axis_index("vert")
    ships = lax.axis_size("ship")
    transes = lax.axis_size("trans")
    slow_ok = jnp.where(v == 0, s > 0, s < ships - 1)
    role_ok = (slow_ok, s >= 0)
    role_dev = ((s + 2 * v - 1, 1 - v), (s, 1 - v))
    side_ok = (t > 0, t < transes - 1)
    side_t = (t - 1, t + 1)
    edge_x = (7 * v, 7 * (1 - v))
    edge_b = (2 * v, 2 * (1 - v))

    barrier = pltpu.get_barrier_semaphore()
    count = 0
    chip_ok = (s > 0, s < ships - 1)
    chip_s = (s - 1, s + 1)
    met = [(role_ok[role], *role_dev[role]) for role in range(2)] + [(chip_ok[i], chip_s[i], v) for i in range(2)]
    for there, ship, vert in met:
        for ok, tt in ((there, t), (there & side_ok[0], t - 1), (there & side_ok[1], t + 1)):

            @pl.when(ok)
            def _():
                pl.semaphore_signal(barrier, inc=1, device_id=(ship, tt, vert), device_id_type=MESH)

            count = count + ok.astype(jnp.int32)
    for side in range(2):

        @pl.when(side_ok[side])
        def _():
            pl.semaphore_signal(barrier, inc=1, device_id=(s, side_t[side], v), device_id_type=MESH)

        count = count + side_ok[side].astype(jnp.int32)

    @pl.when(jnp.logical_not(slow_ok))
    def _():
        far_r[...] = jnp.zeros_like(far_r)
        first_r[...] = jnp.zeros_like(first_r)
        rim_r[2] = jnp.zeros((2, 1, 128), F32)

    for side in range(2):

        @pl.when(jnp.logical_not(side_ok[side]))
        def _():
            for k in range(SWEEPS):
                packs_r[k, side] = jnp.zeros((8, 128), F32)
                diag_r[k, 1, side] = jnp.zeros((1, 128), F32)

        @pl.when(jnp.logical_not(slow_ok & side_ok[side]))
        def _():
            rim_r[side] = jnp.zeros((2, 1, 128), F32)
            for core in range(2):
                prof_r[core, side] = jnp.zeros((1, 128), F32)
            for k in range(SWEEPS):
                diag_r[k, 0, side] = jnp.zeros((1, 128), F32)

    own = pl.ds(pl.multiple_of(8 * v, 8), 8)
    other = pl.ds(pl.multiple_of(8 * (1 - v), 8), 8)
    levels = pl.ds(32 * v, 32)
    whole_slab = pltpu.make_async_copy(pot_hbm, slab, lsem.at[7])
    whole_slab.start()
    local = [
        pltpu.make_async_copy(pot_hbm.at[:, own], pot.at[levels], lsem.at[0]),
        pltpu.make_async_copy(hull_hbm, hullm, lsem.at[1]),
        pltpu.make_async_copy(surf_hbm, surf, lsem.at[2]),
        pltpu.make_async_copy(sten_hbm.at[:, :, own], sten.at[:, levels], lsem.at[3]),
        pltpu.make_async_copy(src_hbm.at[:, own], srcl.at[levels], lsem.at[4]),
        pltpu.make_async_copy(elev_hbm, elev, lsem.at[5]),
        pltpu.make_async_copy(cinv_hbm, cinv, lsem.at[6]),
    ]
    for copy in local:
        copy.start()

    lane = lax.broadcasted_iota(jnp.int32, (8, 128), 1)
    sub = lax.broadcasted_iota(jnp.int32, (8, 128), 0)

    def line_copy(dirn, core):
        return pltpu.make_async_remote_copy(
            line_s.at[dirn], first_r.at[pl.ds(pl.multiple_of(32 * core, 32), 32)],
            line_ss.at[dirn], line_rs.at[core],
            device_id=(chip_s[dirn], t, 1 - dirn), device_id_type=MESH,
        )

    def prof_copy(dirn, side, core):
        return pltpu.make_async_remote_copy(
            prof_s.at[dirn, side], prof_r.at[core, 1 - side],
            prof_ss.at[dirn, side], prof_rs.at[core, 1 - side],
            device_id=(chip_s[dirn], side_t[side], 1 - dirn), device_id_type=MESH,
        )

    def rim_copy(place):
        return pltpu.make_async_remote_copy(
            rim_s, rim_r.at[(1, 0, 2)[place]], rim_ss.at[place], rim_rs.at[(1, 0, 2)[place]],
            device_id=(role_dev[0][0], (side_t + (t,))[place], role_dev[0][1]), device_id_type=MESH,
        )

    rim_ok = (slow_ok & side_ok[0], slow_ok & side_ok[1], slow_ok)
    whole_slab.wait()
    first, last = slab[:, 0, :], slab[:, 15, :]
    line_s[0] = first
    line_s[1] = last
    turned = jnp.transpose(jnp.concatenate([first, last, jnp.zeros((64, 128), F32)], axis=0))
    for end, at in enumerate((0, 127)):
        profile = turned[at : at + 1]
        prof_s[0, end] = pltpu.roll(profile, 8 + 32 * v, 1)
        prof_s[1, end] = pltpu.roll(profile, (104 + 32 * v) % 128, 1)
    local[1].wait()
    local[2].wait()
    hull[...] = hullm[...].astype(F32)
    top[...] = (1.0 - hull[...]) * surf[...]
    rim_s[0] = hull[pl.ds(edge_x[0], 1), :]
    rim_s[1] = top[pl.ds(edge_x[0], 1), :]

    pl.semaphore_wait(barrier, count)

    for dirn in range(2):

        @pl.when(chip_ok[dirn])
        def _():
            line_copy(dirn, v).start()

        for side in range(2):

            @pl.when(chip_ok[dirn] & side_ok[side])
            def _():
                prof_copy(dirn, side, v).start()

    for place in range(3):

        @pl.when(rim_ok[place])
        def _():
            rim_copy(place).start()

    partner = (s, t, 1 - v)
    cross = [
        pltpu.make_async_remote_copy(
            src, dst, xs_sem.at[i], xr_sem.at[i], device_id=partner, device_id_type=MESH
        )
        for i, (src, dst) in enumerate(
            (
                (pot_hbm.at[:, other], pot.at[levels]),
                (sten_hbm.at[:, :, other], sten.at[:, levels]),
                (src_hbm.at[:, other], srcl.at[levels]),
            )
        )
    ]
    for copy in cross:
        copy.start()

    def row_copy(k, role):
        src, dst = ((far_s.at[k], far_r.at[k]), (near_s.at[k], near_r.at[k]))[role]
        return pltpu.make_async_remote_copy(
            src, dst, row_ss.at[k, role], row_rs.at[k, role],
            device_id=(role_dev[role][0], t, role_dev[role][1]), device_id_type=MESH,
        )

    def pack_copy(k, side):
        return pltpu.make_async_remote_copy(
            packs_s.at[k, side], packs_r.at[k, 1 - side], pack_ss.at[k, side], pack_rs.at[k, 1 - side],
            device_id=(s, side_t[side], v), device_id_type=MESH,
        )

    def diag_copy(k, role, side):
        return pltpu.make_async_remote_copy(
            diag_s.at[k, role, side], diag_r.at[k, role, 1 - side],
            diag_ss.at[k, role, side], diag_rs.at[k, role, 1 - side],
            device_id=(role_dev[role][0], side_t[side], role_dev[role][1]), device_id_type=MESH,
        )

    def send_row(k, role, line, top_line):
        whole = jnp.concatenate(
            [
                jnp.broadcast_to(line[0:1], (8, 128)),
                line,
                jnp.broadcast_to(top_line, (8, 128)),
                jnp.zeros((48, 128), F32),
            ],
            axis=0,
        )
        if role == 0:
            sent = (line - far_sent[...]).astype(BF16)
            far_s[k] = sent
            far_sent[...] = far_sent[...] + sent.astype(F32)
        else:
            near_s[k] = whole[8:80]

        turned = jnp.transpose(whole)
        diag_s[k, role, 0] = turned[0:1]
        diag_s[k, role, 1] = turned[127:128]
        for side in range(2):

            @pl.when(role_ok[role] & side_ok[side])
            def _():
                diag_copy(k, role, side).start()

        @pl.when(role_ok[role])
        def _():
            row_copy(k, role).start()

    def send_packs(k):
        left = jnp.zeros((8, 128), F32)
        right = left
        for z in range(65):
            turned = pltpu.roll(field[8 * z + 8 : 8 * z + 16, :], z, 1)
            left = jnp.where(lane == z, turned, left)
            right = jnp.where(lane == (z + 127) % 128, turned, right)
        packs_s[k, 0] = left
        packs_s[k, 1] = pltpu.roll(right, 1, 1)
        for side in range(2):

            @pl.when(side_ok[side])
            def _():
                pack_copy(k, side).start()

    def close_field():
        field[0:8, :] = field[8:16, :]
        field[520:528, :] = hull[...] * field[512:520, :] + top[...]

    def column(ref, x, first):
        return ref[pl.ds(x + first, 64, stride=8), :]

    def widen(core):
        def one(o, _):
            for i in range(4):
                at = 32 * core + 8 * i
                coef[o, pl.ds(pl.multiple_of(8 * at, 64), 64), :] = (
                    sten[o, pl.ds(at, 8)].astype(F32).reshape(64, 128)
                )
            return 0

        lax.fori_loop(0, 27, one, 0)

    far_sent[...] = jnp.zeros((64, 128), F32)
    far_got[...] = jnp.zeros((64, 128), F32)

    local[5].wait()
    local[6].wait()
    weight[...] = 0.5 * (1.0 + elev[...]) * (1.0 + elev[...])
    both = cinv[...].reshape(128, 64)
    high = both.astype(BF16).astype(F32)
    lhs[...] = jnp.concatenate([high, high, both - high], axis=1).astype(BF16)
    local[3].wait()
    widen(v)

    local[0].wait()
    cross[0].wait_recv()
    field[8:520, :] = pot[...].reshape(512, 128)
    close_field()
    send_row(0, 1, column(field, edge_x[1], 8), field[pl.ds(edge_x[1] + 520, 1), :])
    send_packs(0)

    local[4].wait()
    cross[2].wait_recv()
    applied[...] = srcl[...].reshape(512, 128)
    for x in range(8):
        resid[x] = column(applied, x, 0)
        corr[x] = jnp.zeros((64, 128), F32)
    cross[1].wait_recv()
    widen(1 - v)
    for role in range(2):
        for a in range(3):
            for c in range(3):
                o = 9 * a + 3 * edge_b[role] + c
                edge[role, 3 * a + c] = coef[o, pl.ds(edge_x[role], 64, stride=8), :]

    def solve(u, hull_line):
        hi = u.astype(BF16)
        lo = (u - hi.astype(F32)).astype(BF16)
        y = jnp.dot(lhs[...], jnp.concatenate([hi, lo, hi], axis=0), preferred_element_type=F32)
        return jnp.where(hull_line > 0.5, y[64:128], y[0:64])

    lane80 = lax.broadcasted_iota(jnp.int32, (80, 128), 1)

    def gather_first():
        for core in range(2):

            @pl.when(slow_ok)
            def _():
                line_copy(0, core).wait_recv()

            for side in range(2):

                @pl.when(slow_ok & side_ok[side])
                def _():
                    prof_copy(0, 1 - side, core).wait_recv()

        for place in range(3):

            @pl.when(rim_ok[place])
            def _():
                rim_copy((1, 0, 2)[place]).wait_recv()

        for side in range(2):
            level = jnp.where(lane[0:1] < 40, prof_r[0, side], prof_r[1, side])
            level = jnp.where(lane[0:1] == 7, pltpu.roll(level, 127, 1), level)
            turn = (73, 72)[side]
            rim_hull = pltpu.roll(rim_r[side, 0], turn, 1)
            rim_top = pltpu.roll(rim_r[side, 1], turn, 1)
            diag_r[0, 0, side] = jnp.where(lane[0:1] == 72, rim_hull * pltpu.roll(level, 1, 1) + rim_top, level)
        ghost3[1, 8:72, :] = first_r[...]
        ghost3[1, 72:80, :] = jnp.broadcast_to(rim_r[2, 0] * first_r[63:64, :] + rim_r[2, 1], (8, 128))

    def ghost_part(k, role):
        here = role_ok[role] & (k > 0) if role == 0 else role_ok[role]

        @pl.when(here)
        def _():
            row_copy(k, role).wait_recv()

        for side in range(2):

            @pl.when(here & side_ok[side])
            def _():
                diag_copy(k, role, 1 - side).wait_recv()

        if role == 0:

            @pl.when(k == 0)
            def _():
                gather_first()

            @pl.when(k > 0)
            def _():
                line = far_got[...] + far_r[k].astype(F32)
                far_got[...] = line
                ghost3[1, 8:72, :] = line
                ghost3[1, 72:80, :] = jnp.broadcast_to(rim_r[2, 0] * line[63:64], (8, 128))

        else:
            ghost3[1, 8:80, :] = near_r[k]
        ghost3[1, 0:8, :] = jnp.broadcast_to(ghost3[1, 8:9, :], (8, 128))
        line = ghost3[1]
        turned = jnp.transpose(
            jnp.concatenate([diag_r[k, role, 0], diag_r[k, role, 1], jnp.zeros((126, 128), F32)], axis=0)
        )
        ghost3[0] = jnp.where(lane80 == 0, turned[0:80, 0:1], pltpu.roll(line, 1, 1))
        ghost3[2] = jnp.where(lane80 == 127, turned[0:80, 1:2], pltpu.roll(line, 127, 1))
        total = jnp.zeros((64, 128), F32)
        for a in range(3):
            for c in range(3):
                total = total + edge[role, 3 * a + c] * ghost3[c, 7 + a : 71 + a, :]
        return total

    def out_copies(i, hbm):
        mine = pltpu.make_async_copy(outl.at[i, levels], hbm.at[:, own], out_ls.at[i])
        theirs = pltpu.make_async_remote_copy(
            outl.at[i, pl.ds(32 * (1 - v), 32)], hbm.at[:, own], out_ss.at[i], out_rs.at[i],
            device_id=partner, device_id_type=MESH,
        )
        return mine, theirs

    tail_copy = pltpu.make_async_remote_copy(
        tail.at[pl.ds(pl.multiple_of(32 * (1 - v), 32), 32)], tail_r, tail_ss, tail_rs,
        device_id=partner, device_id_type=MESH,
    )

    def sweep(k, _):
        for side in range(2):

            @pl.when(side_ok[side])
            def _():
                pack_copy(k, 1 - side).wait_recv()

        from_left = packs_r[k, 0]
        from_right = packs_r[k, 1]

        def shift(z, _):
            here = pl.ds(pl.multiple_of(8 * z, 8), 8)
            level = jnp.clip(z - 1, 0, 64)
            middle = field[here, :]
            left = jnp.where(lane == 0, pltpu.roll(from_left, (128 - level) % 128, 1), pltpu.roll(middle, 1, 1))
            right = jnp.where(lane == 127, pltpu.roll(from_right, 127 - level, 1), pltpu.roll(middle, 127, 1))
            for c, value in enumerate((left, middle, right)):
                shifted[c, here, :] = jnp.where(sub == 0, 0.0, pltpu.roll(value, 1, 0))
                shifted[3 + c, here, :] = value
                shifted[6 + c, here, :] = jnp.where(sub == 7, 0.0, pltpu.roll(value, 7, 0))
            return 0

        lax.fori_loop(0, 66, shift, 0, unroll=11)

        def block(i, _):
            at = pl.multiple_of(64 * i, 64)
            total = jnp.zeros((64, 128), F32)
            for b in range(3):
                for c in range(3):
                    window = shifted[3 * b + c, pl.ds(at, 80), :]
                    for a in range(3):
                        total = total + coef[9 * a + 3 * b + c, pl.ds(at, 64), :] * window[8 * a : 8 * a + 64]
            applied[pl.ds(at, 64), :] = total
            return 0

        lax.fori_loop(0, 8, block, 0)

        part = ghost_part(k, 1)
        resid_x = edge_x[1]
        applied[pl.ds(resid_x, 64, stride=8), :] = column(applied, resid_x, 0) + part

        for pair in range(4):
            lines = []
            for x in (2 * pair, 2 * pair + 1):
                u = resid[x] - column(applied, x, 0)

                @pl.when(k == 0)
                def _():
                    resid[x] = u

                lines.append(u)
            u = jnp.concatenate(lines, axis=1)
            mask = jnp.concatenate([hull[2 * pair : 2 * pair + 1], hull[2 * pair + 1 : 2 * pair + 2]], axis=1)
            step = solve(u, mask)
            for i, x in enumerate((2 * pair, 2 * pair + 1)):
                corr[x] = corr[x] + weight[x : x + 1] * step[:, 128 * i : 128 * i + 128]

        @pl.when(k < SWEEPS - 1)
        def _():
            line = corr[edge_x[1]]
            send_row(k + 1, 1, line, hull[pl.ds(edge_x[1], 1), :] * line[63:64])

        @pl.when(k == SWEEPS - 1)
        def _():
            for x in range(8):
                field[pl.ds(8 + x, 64, stride=8), :] = corr[x]
            applied[...] = pot[...].reshape(512, 128) + field[8:520, :]
            outl[1] = applied[...].reshape(64, 8, 128)
            for copy in out_copies(1, upd_hbm):
                copy.start()

        part = ghost_part(k, 0)
        x = edge_x[0]

        @pl.when(k == 0)
        def _():
            resid[x] = resid[x] - part
            top[...] = jnp.zeros((8, 128), F32)

        line_hull = hull[pl.ds(x, 1), :]
        change = weight[pl.ds(x, 1), :] * solve(part, line_hull)
        line = corr[x] - change
        corr[x] = line

        @pl.when(k == SWEEPS - 1)
        def _():
            tail[...] = column(applied, x, 0) - change
            tail_copy.start()

        @pl.when(k < SWEEPS - 1)
        def _():
            send_row(k + 1, 0, line, line_hull * line[63:64])

        @pl.when(k < SWEEPS - 1)
        def _():
            for x in range(8):
                field[pl.ds(8 + x, 64, stride=8), :] = corr[x]
            close_field()
            send_packs(k + 1)

        @pl.when(k == 0)
        def _():
            for x in range(8):
                applied[pl.ds(x, 64, stride=8), :] = resid[x]
            outl[0] = applied[...].reshape(64, 8, 128)
            for copy in out_copies(0, res_hbm):
                copy.start()

        return 0

    lax.fori_loop(0, SWEEPS, sweep, 0)

    for copy in cross:
        copy.wait_send()

    def drain(k, _):
        for role in range(2):
            sent = role_ok[role] & (k > 0) if role == 0 else role_ok[role]

            @pl.when(sent)
            def _():
                row_copy(k, role).wait_send()

            @pl.when(side_ok[role])
            def _():
                pack_copy(k, role).wait_send()

            for side in range(2):

                @pl.when(sent & side_ok[side])
                def _():
                    diag_copy(k, role, side).wait_send()

        return 0

    lax.fori_loop(0, SWEEPS, drain, 0)
    for dirn in range(2):

        @pl.when(chip_ok[dirn])
        def _():
            line_copy(dirn, v).wait_send()

        for side in range(2):

            @pl.when(chip_ok[dirn] & side_ok[side])
            def _():
                prof_copy(dirn, side, v).wait_send()

    for place in range(3):

        @pl.when(rim_ok[place])
        def _():
            rim_copy(place).wait_send()

    for i, hbm in enumerate((res_hbm, upd_hbm)):
        mine, theirs = out_copies(i, hbm)
        mine.wait()
        theirs.wait_send()
        pltpu.make_async_remote_copy(
            outl.at[i, levels], hbm.at[:, other], out_ss.at[i], out_rs.at[i],
            device_id=partner, device_id_type=MESH,
        ).wait_recv()
    slab_rows = upd_hbm.reshape(512, 128)
    slab_rows[pl.ds(15 * v, 32, stride=16), :] = tail[pl.ds(pl.multiple_of(32 * v, 32), 32), :]
    tail_copy.wait_recv()
    slab_rows[pl.ds(15 * (1 - v), 32, stride=16), :] = tail_r[...]
    tail_copy.wait_send()


def store(upd_vmem, res_vmem, upd_hbm, res_hbm, sem):
    copies = [
        pltpu.make_async_copy(upd_vmem, upd_hbm, sem.at[0]),
        pltpu.make_async_copy(res_vmem, res_hbm, sem.at[1]),
    ]
    for copy in copies:
        copy.start()
    for copy in copies:
        copy.wait()


def per_device(potential, source, stencil, surface_potential, elevation, hull_mask, column_inverse):
    vm = pltpu.VMEM
    dma = pltpu.SemaphoreType.DMA
    n = SWEEPS
    held = pl.pallas_call(
        kernel,
        out_shape=(vm((32, 16, 128), F32), vm((32, 16, 128), F32)),
        in_specs=[pl.BlockSpec(memory_space=pl.ANY)] * 7,
        out_specs=(pl.BlockSpec(memory_space=pltpu.VMEM), pl.BlockSpec(memory_space=pltpu.VMEM)),
        scratch_shapes=[
            vm((64, 8, 128), F32), vm((64, 8, 128), F32), vm((27, 64, 8, 128), BF16), vm((8, 128), F32), vm((8, 128), F32),
            vm((8, 128), jnp.int32), vm((2, 64, 64), F32),
            vm((27, 512, 128), F32), vm((2, 9, 64, 128), F32), vm((9, 528, 128), F32), vm((528, 128), F32), vm((512, 128), F32),
            vm((8, 64, 128), F32), vm((8, 64, 128), F32), vm((8, 128), F32), vm((8, 128), F32), vm((8, 128), F32), vm((128, 192), BF16),
            vm((3, 80, 128), F32), vm((2, 64, 8, 128), F32),
            vm((n, 64, 128), BF16), vm((n, 64, 128), BF16), vm((64, 128), F32), vm((64, 128), F32), vm((64, 128), F32), vm((n, 72, 128), F32), vm((n, 72, 128), F32),
            vm((n, 2, 8, 128), F32), vm((n, 2, 8, 128), F32), vm((n, 2, 2, 1, 128), F32), vm((n, 2, 2, 1, 128), F32),
            vm((64, 128), F32), vm((32, 128), F32), vm((32, 16, 128), F32), vm((2, 32, 128), F32), vm((2, 2, 1, 128), F32), vm((2, 2, 1, 128), F32), vm((2, 1, 128), F32),
            vm((3, 2, 1, 128), F32),
            dma(()), dma(()), dma((2,)), dma((2,)), dma((2, 2)), dma((2, 2)), dma((3,)), dma((3,)),
            dma((8,)), dma((3,)), dma((3,)), dma((n, 2)), dma((n, 2)), dma((n, 2)), dma((n, 2)), dma((n, 2, 2)), dma((n, 2, 2)),
            dma((2,)), dma((2,)), dma((2,)),
        ],
        compiler_params=pltpu.CompilerParams(collective_id=0, has_side_effects=True, vmem_limit_bytes=60 * 1024 * 1024),
        name="defect_correction",
    )(potential, source, stencil, surface_potential, elevation, hull_mask, column_inverse)
    return pl.pallas_call(
        store,
        out_shape=(jax.ShapeDtypeStruct((32, 16, 128), F32), jax.ShapeDtypeStruct((32, 16, 128), F32)),
        in_specs=[pl.BlockSpec(memory_space=pltpu.VMEM)] * 2,
        out_specs=(pl.BlockSpec(memory_space=pl.ANY), pl.BlockSpec(memory_space=pl.ANY)),
        scratch_shapes=[dma((2,))],
        name="store",
    )(*[pltpu.with_memory_space_constraint(x, pltpu.VMEM) for x in held])


def solution(mesh):
    return jax.shard_map(
        per_device,
        mesh=mesh,
        in_specs=(
            P("vert", "ship", "trans"),
            P("vert", "ship", "trans"),
            P(None, "vert", "ship", "trans"),
            P(("ship", "vert"), "trans"),
            P(("ship", "vert"), "trans"),
            P(("ship", "vert"), "trans"),
            P(),
        ),
        out_specs=(P("vert", "ship", "trans"), P("vert", "ship", "trans")),
        check_vma=False,
    )
```
